32 devices in a mesh: scen: 8 (over z, x), row: 2 (over core), col: 2 (over y).
Axes of the slice: x: 2, y: 2, z: 4, core: 2. Of those that a mesh axis runs over, the one named last changes fastest.
Arguments:
- kkt: float32 [24, 768, 768], P('scen', ('row', 'col')), as said below
- border: float32 [24, 768, 4096], P('scen', None, ('row', 'col')), may hold values from -0.21875 to 0.21875
- first_diag: float32 [4096], P('scen'), may hold values from 0.5 to 1.5
- assignment: int32 [24], P('scen'), may hold values from 0 to 23, as said below
- panel: int32 [8], replicated, may hold values from 0 to 7, each once
Outputs:
- schur: float32 [4096, 4096], P('scen', ('row', 'col'))
- panel_factor: float32 [4096, 512], P('scen', ('row', 'col'))
The draws below stay inside these ranges and needn't reach their ends.
Inputs may be any that keep to these rules, and one draw needn't show every extreme that they name: assignment is a permutation; with k = d * 3 + j (0 <= j < 3), assignment[k] is either k or (d XOR 1) * 3 + j, and the two scenarios of such a pair are either both fixed or swapped. panel is a permutation. Each kkt block is symmetric positive definite; after scaling by its diagonal, the off-diagonal part has spectral norm about one half.
All inputs are finite; a program needn't handle non-finite values.
Results may differ from the reference program's by a relative error of at most 0.00015.
Values sent between devices are 32-bit elements; how exact they have to be, the bound alone decides.
A program may use at most 192 MiB of HBM per device.

```python
import math
import jax
import jax.numpy as jnp
from jax import lax

NK = 768
NF = 4096
PW = 512
NEWTON = 3
S_DEV = 3
NSCEN = 24


def draw_kkt(key, part):
    first_key, second_key, third_key = jax.random.split(jax.random.fold_in(key, 11), 3)
    entry_scale = jnp.exp(jax.random.uniform(first_key, (NSCEN, NK), minval=math.log(0.5), maxval=math.log(4.0)))
    scen_scale = jnp.exp(jax.random.uniform(third_key, (NSCEN, 1), minval=math.log(0.5), maxval=math.log(4.0)))
    scales = entry_scale * scen_scale
    noise = jax.random.normal(second_key, (NSCEN, NK, NK))
    paired = (noise + jnp.swapaxes(noise, 1, 2)) * (0.25 / math.sqrt(2.0 * NK))
    paired = paired * (1.0 - jnp.eye(NK, dtype=jnp.float32))[None]
    roots = jnp.sqrt(scales)
    blocks = roots[:, :, None] * paired * roots[:, None, :]
    blocks = blocks + jnp.eye(NK, dtype=jnp.float32)[None] * scales[:, :, None]
    return blocks.astype(jnp.float32)


def draw_assignment(key, part):
    groups = NSCEN // S_DEV
    flips = jax.random.randint(jax.random.fold_in(key, 23), (groups // 2, S_DEV), 0, 2)
    flips = jnp.repeat(flips, 2, axis=0)
    device_ids = jnp.arange(groups, dtype=jnp.int32)[:, None]
    slot_ids = jnp.arange(S_DEV, dtype=jnp.int32)[None, :]
    own = device_ids * S_DEV + slot_ids
    other = (device_ids + 1 - 2 * (device_ids % 2)) * S_DEV + slot_ids
    chosen = jnp.where(flips == 1, other, own)
    return chosen.reshape(-1).astype(jnp.int32)


def block_levels(key, extent, cuts, low, high):
    loudness, own = 1.0, jax.random.fold_in(key, 6)
    for position, parts in cuts:
        draws = jnp.exp(jax.random.uniform(jax.random.fold_in(own, position), (parts,), jnp.float32, low / len(cuts), high / len(cuts)))
        loudness = loudness * jnp.repeat(draws, extent[position] // parts).reshape([-1 if axis == position else 1 for axis in range(len(extent))])
    return loudness


def bell_draw(stream_key, dims, scale, most, shards=(), kind=jnp.bfloat16):
    loudness = block_levels(stream_key, dims, shards, -0.22, 0.18) if shards else 1.0
    array = jax.random.normal(stream_key, dims, jnp.float32) * scale * loudness
    return jnp.minimum(jnp.maximum(array, -most), most).astype(kind)


def setup_inputs(seed: int = 0) -> dict:
    keys = jax.random.split(jax.random.key(seed), 6)
    kkt = draw_kkt(jax.random.fold_in(keys[5], 71), 0)
    border = bell_draw(keys[1], (NSCEN, NK, NF), (2.0 * (NK * NSCEN) ** -0.5), 0.21875, ((0, 8), (2, 4)), jnp.float32)
    first_diag = jnp.clip(0.5 + 1.0 * jax.random.uniform(keys[2], (NF,), jnp.float32) ** block_levels(keys[2], (NF,), ((0, 8),), -0.2, 0.2), 0.5, 1.5)
    assignment = draw_assignment(jax.random.fold_in(keys[5], 71), 0)
    panel = jax.random.permutation(keys[4], NF // PW).astype(jnp.int32)
    return {"kkt": kkt, "border": border, "first_diag": first_diag, "assignment": assignment, "panel": panel}


HIGH = lax.Precision.HIGHEST

def invert(kkt_block):
    inv_diag = 1.0 / jnp.diagonal(kkt_block)
    approx = jnp.diag(inv_diag)
    for step in range(NEWTON):
        left = jnp.dot(approx.astype(jnp.float32), kkt_block.astype(jnp.float32), precision=HIGH, preferred_element_type=jnp.float32)
        approx = 2.0 * approx - jnp.dot(left.astype(jnp.float32), approx.astype(jnp.float32), precision=HIGH, preferred_element_type=jnp.float32)
    return approx

def reference(kkt, border, first_diag, assignment, panel):
    start_schur = jnp.diag(first_diag)

    def add_scenario(index, schur):
        block = lax.dynamic_index_in_dim(kkt, index, 0, keepdims=False)
        approx = invert(block)
        chosen = lax.dynamic_index_in_dim(border, assignment[index], 0, keepdims=False)
        solved = jnp.dot(approx.astype(jnp.float32), chosen.astype(jnp.float32), precision=HIGH, preferred_element_type=jnp.float32)
        return schur + lax.dot_general(chosen.astype(jnp.float32), solved.astype(jnp.float32), (((0,), (0,)), ((), ())), precision=HIGH, preferred_element_type=jnp.float32)
    schur = lax.fori_loop(0, NSCEN, add_scenario, start_schur)
    start = panel[0] * PW
    columns = lax.dynamic_slice_in_dim(schur, start, PW, 1)
    block = lax.dynamic_slice_in_dim(columns, start, PW, 0)
    symmetric = 0.5 * (block + block.T)
    lower_factor = jnp.linalg.cholesky(symmetric)
    factor = lax.linalg.triangular_solve(lower_factor, columns, left_side=False, lower=True, transpose_a=True)
    return (schur, factor)
```

```python
import jax
import jax.numpy as jnp
from jax import lax
from jax.sharding import PartitionSpec as P

PW = 512
NEWTON = 3


HIGH = lax.Precision.HIGH
GROUP = ("row", "col")


def swapped(value, axis, distance):
    mask = 2**distance
    pairs = [(source, source ^ mask) for source in range(lax.axis_size(axis))]
    return lax.ppermute(value, axis, pairs)


def gathered_rows(value, axis):
    count = lax.axis_size(axis)
    index = lax.axis_index(axis)
    rows = value.shape[1]
    whole = jnp.zeros((value.shape[0], rows * count, value.shape[2]), value.dtype)
    whole = lax.dynamic_update_slice_in_dim(whole, value, index * rows, 1)
    for shift in range(1, count):
        pairs = [(source, (source + shift) % count) for source in range(count)]
        origin = lax.rem(index - shift + count, count)
        whole = lax.dynamic_update_slice_in_dim(
            whole, lax.ppermute(value, axis, pairs), origin * rows, 1
        )
    return whole


def matmul(left, right, precision=HIGH):
    return jnp.dot(left, right, precision=precision, preferred_element_type=jnp.float32)


def contract(left, right):
    return lax.dot_general(
        left, right, (((0,), (0,)), ((), ())), precision=HIGH, preferred_element_type=jnp.float32
    )


def body(kkt, border, first_diag, assignment, panel):
    scen_index = lax.axis_index("scen")
    own_index = lax.axis_index(GROUP)
    group_size = lax.axis_size(GROUP)
    slots, order, col_count = border.shape
    width = col_count * group_size
    scenario_ids = scen_index * slots + jnp.arange(slots, dtype=jnp.int32)
    kkt = jnp.where((assignment == scenario_ids)[:, None, None], kkt, swapped(kkt, "scen", 0))
    kkt_all = gathered_rows(gathered_rows(kkt, "col"), "row")
    gathered = lax.all_gather(border, GROUP, axis=2, tiled=True)
    eye = jnp.eye(order, dtype=jnp.bool_)
    inverses = []
    for slot in range(slots):
        full = kkt_all[slot]
        diag = jnp.where(eye, full, 0.0)
        row_inv = 1.0 / jnp.sum(diag, axis=1, keepdims=True)
        col_inv = 1.0 / jnp.sum(diag, axis=0, keepdims=True)
        approx = jnp.where(eye, 2.0 * row_inv, 0.0) - row_inv * full * col_inv
        for step in range(NEWTON - 1):
            approx = 2.0 * approx - matmul(matmul(approx, full), approx)
        inverses.append(approx)
    solved = jnp.concatenate([matmul(inverses[slot], border[slot]) for slot in range(slots)], 0)
    border_all = gathered.reshape(slots * order, width)

    panel_start = panel[0] * PW
    share = PW // group_size
    own_start = panel_start + own_index * share

    share_solved = jnp.concatenate(
        [
            matmul(inverses[slot], lax.dynamic_slice_in_dim(gathered[slot], own_start, share, 1))
            for slot in range(slots)
        ],
        0,
    )
    panel_border = lax.dynamic_slice_in_dim(border_all, panel_start, PW, 1)
    block = contract(panel_border, share_solved)
    row_span = first_diag.shape[0]
    global_rows = scen_index * row_span + jnp.arange(row_span, dtype=jnp.int32)
    share_ids = own_start + jnp.arange(share, dtype=jnp.int32)
    owned = global_rows[:, None] == share_ids[None, :]
    share_diag = jnp.sum(jnp.where(owned, first_diag[:, None], 0.0), axis=0)
    panel_ids = panel_start + jnp.arange(PW, dtype=jnp.int32)
    block = block + jnp.where(panel_ids[:, None] == share_ids[None, :], share_diag[None, :], 0.0)
    block = lax.psum(block, "scen")
    block = lax.all_gather(block, GROUP, axis=1, tiled=True)
    symmetric = 0.5 * (block + block.T)
    lower_factor = jnp.linalg.cholesky(symmetric)
    lower_inverse = lax.linalg.triangular_solve(
        lower_factor, jnp.eye(PW, dtype=jnp.float32), left_side=True, lower=True
    )
    own_inverse = lax.dynamic_slice_in_dim(lower_inverse, own_index * share, share, 0)

    def schur_columns(start, count, solved):
        tile = contract(border_all, lax.dynamic_slice_in_dim(solved, start, count, 1))
        summed = lax.psum_scatter(tile, "scen", scatter_dimension=0, tiled=True)
        global_cols = own_index * col_count + start + jnp.arange(count, dtype=jnp.int32)
        on_diag = global_rows[:, None] == global_cols[None, :]
        return summed + jnp.where(on_diag, first_diag[:, None], 0.0)

    if col_count >= PW:
        pieces = col_count // PW
        first = lax.rem(panel[0], pieces)
        schur = jnp.zeros((row_span, col_count), jnp.float32)
        panel_rows = None
        for piece in range(pieces):
            start = lax.rem(first + piece, pieces) * PW
            columns = schur_columns(start, PW, solved)
            if piece == 0:
                owns = own_index == panel[0] // pieces
                columns, solved = lax.optimization_barrier((columns, solved))
                panel_rows = lax.psum(jnp.where(owns, columns, 0.0), GROUP)
            schur = lax.dynamic_update_slice_in_dim(schur, columns, start, 1)
    else:
        schur = schur_columns(jnp.int32(0), col_count, solved)
        parts = PW // col_count
        position = own_index - panel[0] * parts
        owns = (position >= 0) & (position < parts)
        placed = jnp.zeros((row_span, PW), jnp.float32)
        placed = lax.dynamic_update_slice_in_dim(
            placed, jnp.where(owns, schur, 0.0), jnp.clip(position, 0, parts - 1) * col_count, 1
        )
        panel_rows = lax.psum(placed, GROUP)
    own_cols = lax.dot_general(
        panel_rows,
        own_inverse,
        (((1,), (1,)), ((), ())),
        precision=lax.Precision.HIGHEST,
        preferred_element_type=jnp.float32,
    )
    return (schur, own_cols)


def solution(mesh):
    in_specs = (
        P("scen", ("row", "col"), None),
        P("scen", None, ("row", "col")),
        P("scen"),
        P("scen"),
        P(),
    )
    out_specs = (P("scen", ("row", "col")), P("scen", ("row", "col")))
    return jax.shard_map(body, mesh=mesh, in_specs=in_specs, out_specs=out_specs, check_vma=False)
```
